32 devices in a mesh: seq: 16 (over z, x, core), head: 1, grp: 2 (over y).
Axes of the slice: x: 2, y: 2, z: 4, core: 2. Of those that a mesh axis runs over, the one named last changes fastest.
Arguments:
- queries: bfloat16 [4096, 1024], P(('seq', 'grp'), 'head'), may hold values from -54 to 54
- grad_out: bfloat16 [4096, 1024], P(('seq', 'grp'), 'head'), may hold values from -48 to 48
- states: bfloat16 [4096, 8192], P(('seq', 'grp'), 'head'), may hold values from -6 to 6
- kv_weight: bfloat16 [8192, 256], P('head'), may hold values from -0.0625 to 0.0625
- query_gain: float32 [128], replicated, may hold values from 0.5 to 2.5
- key_gain: float32 [128], replicated, may hold values from 0.5 to 2.5
- row_tiles: int32 [4096, 2], P(('seq', 'grp')), may hold values from 0 to 4, as said below
Outputs:
- attn_out: bfloat16 [4096, 1024], P(('seq', 'grp'), 'head')
- kv_grad: float32 [4096, 256], P(('seq', 'grp'), 'head')
The draws below stay inside these ranges and needn't reach their ends.
Inputs may be any that keep to these rules, and one draw needn't show every extreme that they name: For each image i there is a first row, never row 0, from which row_tiles[r, i] equals that image's count of valid tiles, 1 to 4, and before which it is 0; these first rows do not fall with i. Some image has all 4 tiles valid.
All inputs are finite; a program needn't handle non-finite values.
Results may differ from the reference program's by a relative error of at most 0.023.
Values may be sent and summed in bfloat16 or wider, within the bound.
No kernel may reach another device: no remote copies, remote signals or barrier semaphores. Data moves between devices by JAX's collectives and lax.ppermute only.
A program may use at most 128 MiB of HBM per device.

```python
import math
import jax
import jax.numpy as jnp
from jax import lax

D = 8192
HEAD_DIM = 128
GROUP = 8
KV_HEADS = 1
HEADS = 8
ROWS = 4096
IMAGES = 2
TILES = 4
TILE_TOK = 512
IMG = 4096


def draw_queries(key, part):
    normal_part = jnp.clip(jax.random.normal(key, (ROWS, HEADS, HEAD_DIM), jnp.float32), -6.0, 6.0)
    return normal_part.reshape(ROWS, HEADS * HEAD_DIM).astype(jnp.bfloat16)


def draw_row_tiles(key, part):
    count_key, first_key, later_key, full_key = jax.random.split(jax.random.fold_in(key, 11), 4)
    tile_counts = jax.random.randint(count_key, (IMAGES,), 1, TILES + 1, jnp.int32)
    full_image = jax.random.randint(full_key, (1,), 0, IMAGES, jnp.int32)
    image_index = jnp.arange(IMAGES, dtype=jnp.int32)
    tile_counts = jnp.where(image_index == full_image, TILES, tile_counts).astype(jnp.int32)
    early_limit = max(ROWS // 8, 2)
    first_row = jax.random.randint(first_key, (1,), 1, early_limit, jnp.int32)
    later_rows = jax.random.randint(later_key, (IMAGES - 1,), early_limit, ROWS, jnp.int32)
    start_rows = jnp.sort(jnp.concatenate([first_row, later_rows]))
    row_index = jnp.arange(ROWS, dtype=jnp.int32)[:, None]
    return jnp.where(row_index >= start_rows[None, :], tile_counts[None, :], 0).astype(jnp.int32)


def level_of(own_key, shape, cuts, least, top_value):
    gain = 1.0
    for axis_at, blocks in cuts:
        steps = jax.random.uniform(jax.random.fold_in(jax.random.fold_in(own_key, 6), axis_at), (blocks,), jnp.float32, least / len(cuts), top_value / len(cuts))
        gain = gain * jnp.repeat(jnp.exp(steps), shape[axis_at] // blocks).reshape((-1,) + (1,) * (len(shape) - 1 - axis_at))
    return gain


def normal_values(key, extent, width, most, cuts=(), kind=jnp.bfloat16):
    factor_of = level_of(key, extent, cuts, -0.22, 0.18) if cuts else 1.0
    entries = jax.random.normal(key, extent, jnp.float32) * width * factor_of
    return jnp.minimum(jnp.maximum(entries, -most), most).astype(kind)


def setup_inputs(seed: int = 0) -> dict:
    seeds = jax.random.split(jax.random.key(seed), 8)
    queries = draw_queries(jax.random.fold_in(seeds[7], 71), 0)
    grad_out = normal_values(seeds[1], (ROWS, HEADS * HEAD_DIM), 8.0, 48.0, ((0, 32),))
    states = normal_values(seeds[2], (IMG, D), 1.0, 6.0, ((0, 32),))
    kv_weight = normal_values(seeds[3], (D, KV_HEADS * 2 * HEAD_DIM), D ** -0.5, 0.0625)
    query_gain = jnp.clip(jnp.exp(jax.random.uniform(seeds[4], (HEAD_DIM,), jnp.float32, math.log(0.5), math.log(2.5))), 0.5, 2.5)
    key_gain = jnp.clip(jnp.exp(jax.random.uniform(seeds[5], (HEAD_DIM,), jnp.float32, math.log(0.5), math.log(2.5))), 0.5, 2.5)
    row_tiles = draw_row_tiles(jax.random.fold_in(seeds[7], 71), 0)
    return {"queries": queries, "grad_out": grad_out, "states": states, "kv_weight": kv_weight, "query_gain": query_gain, "key_gain": key_gain, "row_tiles": row_tiles}


epsilon = 1e-05

def root_mean(values):
    return jnp.sqrt(lax.optimization_barrier(jnp.mean(values * values, axis=-1, keepdims=True)) + epsilon)

def rounded(values):
    return lax.optimization_barrier(values.astype(jnp.bfloat16)).astype(jnp.float32)

def visible(row_tiles):
    tile_index = jnp.arange(TILES, dtype=jnp.int32)
    allowed = tile_index[None, None, :] < row_tiles[:, :, None]
    allowed = jnp.broadcast_to(allowed[:, :, :, None], allowed.shape + (TILE_TOK,))
    return allowed.reshape(row_tiles.shape[0], IMAGES * TILES * TILE_TOK)

def reference(queries, grad_out, states, kv_weight, query_gain, key_gain, row_tiles):
    score_scale = 1.0 / math.sqrt(HEAD_DIM)
    projected = jnp.dot(states, kv_weight, preferred_element_type=jnp.float32)
    projected = projected.reshape(IMG, KV_HEADS, 2, HEAD_DIM)
    keys_raw = projected[:, :, 0]
    key_rms = root_mean(keys_raw)
    keys_normed = lax.optimization_barrier((keys_raw / key_rms * key_gain).astype(jnp.bfloat16))
    value_rows = lax.optimization_barrier(projected[:, :, 1].astype(jnp.bfloat16))
    query_full = queries.astype(jnp.float32).reshape(ROWS, KV_HEADS, GROUP, HEAD_DIM)
    query_hat = lax.optimization_barrier((query_full / root_mean(query_full) * query_gain).astype(jnp.bfloat16))
    cotangent = grad_out.reshape(ROWS, KV_HEADS, GROUP, HEAD_DIM)
    allowed = visible(row_tiles)
    row_live = lax.optimization_barrier(jnp.sum(row_tiles, axis=1)) > 0
    block_rows = min(ROWS, 512)
    block_count = ROWS // block_rows
    mask_blocks = allowed.reshape(block_count, block_rows, IMG)
    live_blocks = row_live.reshape(block_count, block_rows)

    def head_pass(inputs):
        query_head, grad_head, key_head, value_head = inputs
        key_float = key_head.astype(jnp.float32)
        value_float = value_head.astype(jnp.float32)

        def block_step(carry, pieces):
            key_total, value_total = carry
            query_block, grad_block, mask_block, live_block = pieces
            query_float = query_block.astype(jnp.float32)
            grad_float = grad_block.astype(jnp.float32)
            scores = jnp.einsum('rgd,jd->rgj', query_float, key_float) * score_scale
            weights = jnp.where(mask_block[:, None, :], jnp.exp(scores), 0.0)
            weight_total = lax.optimization_barrier(jnp.sum(weights, axis=-1))
            denominator = jnp.where(live_block[:, None], weight_total, 1.0)
            weighted = jnp.einsum('rgj,jd->rgd', rounded(weights), value_float)
            attended = (weighted / denominator[..., None]).astype(jnp.bfloat16)
            probs = weights / denominator[..., None]
            row_delta = lax.optimization_barrier(jnp.sum(grad_float * attended.astype(jnp.float32), axis=-1))
            value_total = value_total + jnp.einsum('rgj,rgd->jd', rounded(probs), grad_float)
            prob_grad = jnp.einsum('rgd,jd->rgj', grad_float, value_float)
            score_grad = rounded(probs * (prob_grad - row_delta[..., None]) * score_scale)
            key_total = key_total + jnp.einsum('rgj,rgd->jd', score_grad, query_float)
            return ((key_total, value_total), attended)
        start_carry = (jnp.zeros((IMG, HEAD_DIM), jnp.float32), jnp.zeros((IMG, HEAD_DIM), jnp.float32))
        query_blocks = query_head.reshape(block_count, block_rows, GROUP, HEAD_DIM)
        grad_blocks = grad_head.reshape(block_count, block_rows, GROUP, HEAD_DIM)
        totals, attended = lax.scan(block_step, start_carry, (query_blocks, grad_blocks, mask_blocks, live_blocks))
        return (totals[0], totals[1], attended)
    key_grad, value_grad, attended = lax.map(head_pass, (query_hat.transpose(1, 0, 2, 3), cotangent.transpose(1, 0, 2, 3), keys_normed.transpose(1, 0, 2), value_rows.transpose(1, 0, 2)))
    attn_out = attended.reshape(KV_HEADS, ROWS, GROUP, HEAD_DIM).transpose(1, 0, 2, 3)
    attn_out = attn_out.reshape(ROWS, HEADS * HEAD_DIM)
    key_grad = key_grad.transpose(1, 0, 2) * key_gain
    value_grad = value_grad.transpose(1, 0, 2)
    raw_grad = key_grad / key_rms - keys_raw * lax.optimization_barrier(jnp.mean(key_grad * keys_raw, axis=-1, keepdims=True)) / key_rms ** 3
    kv_grad = jnp.stack([raw_grad, value_grad], axis=2).reshape(IMG, KV_HEADS * 2 * HEAD_DIM)
    return (attn_out, kv_grad)
```

```python
import functools
import math

import jax
import jax.numpy as jnp
from jax import lax
from jax.experimental import pallas as pl
from jax.experimental.pallas import tpu as pltpu
from jax.sharding import PartitionSpec as P

HEAD_DIM = 128
GROUP = 8
IMAGES = 2
TILES = 4
TILE_TOK = 512
CORES = 2
MID = 2
EPS = 1e-05
LOG2E = 1.0 / math.log(2.0)
HIDDEN = -1e30
F32 = jnp.float32
BF16 = jnp.bfloat16
AXES = ("seq", "grp")


NT = (((1,), (1,)), ((), ()))


def call(kernel, outs, n_in, flops=0, nbytes=0, exps=0, scratch=(), smem=0, **kw):
    vmem = pl.BlockSpec(memory_space=pltpu.VMEM)
    return pl.pallas_call(
        kernel,
        out_shape=outs,
        in_specs=[pl.BlockSpec(memory_space=pltpu.SMEM)] * smem + [vmem] * (n_in - smem),
        out_specs=jax.tree.map(lambda _: vmem, outs),
        scratch_shapes=scratch,
        cost_estimate=pl.CostEstimate(flops=flops, bytes_accessed=nbytes, transcendentals=exps),
        **kw,
    )


def root_mean(values):
    return jnp.sqrt(jnp.mean(values * values, axis=-1, keepdims=True) + EPS)


def norm_kv(proj, gain):
    raw = proj[:, :HEAD_DIM]
    keys = raw / root_mean(raw) * gain
    return jnp.concatenate([keys.astype(BF16), proj[:, HEAD_DIM:].astype(BF16)], axis=1)


def project_kernel(states_ref, weight_ref, gain_ref, kv_ref, raw_ref):
    step = pl.program_id(0)

    @pl.when(step == 0)
    def _():
        raw_ref[...] = jnp.zeros_like(raw_ref)

    raw_ref[...] += jnp.dot(states_ref[...], weight_ref[...], preferred_element_type=F32)

    @pl.when(step == pl.num_programs(0) - 1)
    def _():
        kv_ref[...] = norm_kv(raw_ref[...], gain_ref[...])


def project(states, weight, gain):
    tokens, depth = states.shape
    width = weight.shape[1]
    block = min(depth, 1024)
    return pl.pallas_call(
        project_kernel,
        out_shape=(
            jax.ShapeDtypeStruct((tokens, width), BF16),
            jax.ShapeDtypeStruct((tokens, width), F32),
        ),
        grid=(depth // block,),
        in_specs=[
            pl.BlockSpec((tokens, block), lambda i: (0, i)),
            pl.BlockSpec((block, width), lambda i: (i, 0)),
            pl.BlockSpec((1, HEAD_DIM), lambda i: (0, 0)),
        ],
        out_specs=(
            pl.BlockSpec((tokens, width), lambda i: (0, 0)),
            pl.BlockSpec((tokens, width), lambda i: (0, 0)),
        ),
        cost_estimate=pl.CostEstimate(
            flops=2 * tokens * depth * width,
            bytes_accessed=2 * (tokens + width) * depth,
            transcendentals=0,
        ),
    )(states, weight, gain)


def prep_kernel(q_own, q_par, d_own, d_par, gain_ref, qh_ref, do_ref, dot_ref):
    rows = q_own.shape[0]
    scale = LOG2E / math.sqrt(HEAD_DIM)
    gain = gain_ref[...] * scale
    for part, (q_ref, d_ref) in enumerate(((q_own, d_own), (q_par, d_par))):
        for h in range(GROUP):
            lanes = slice(h * HEAD_DIM, (h + 1) * HEAD_DIM)
            at = h * 2 * rows + part * rows
            q = q_ref[:, lanes].astype(F32)
            qh_ref[at : at + rows, :] = (q / root_mean(q) * gain).astype(BF16)
            d = d_ref[:, lanes]
            do_ref[at : at + rows, :] = d
            dot_ref[lanes, part * rows : (part + 1) * rows] = d.astype(F32).T.astype(BF16)


def fwd_kernel(first, tokens, tiles_ref, kv_ref, qh_ref, b_own, b_par, *refs):
    if first:
        wt_ref, acc_ref, den_ref = refs
    else:
        acc_in, den_in, wt_ref, acc_ref, den_ref = refs
    rows = qh_ref.shape[0] // GROUP
    keys = kv_ref[:, :HEAD_DIM]
    values_t = kv_ref[:, HEAD_DIM:].astype(F32).T.astype(BF16)
    blocks = kv_ref.shape[0] // tokens
    bias = []
    for i in range(blocks):
        row = pl.ds(tiles_ref[i], 1)
        bias.append(jnp.concatenate([b_own[row, :], b_par[row, :]], axis=1))
    for h in range(GROUP):
        q = qh_ref[h * rows : (h + 1) * rows, :]
        lanes = slice(h * rows, (h + 1) * rows)
        total = jnp.zeros((1, rows), F32)
        for i in range(blocks):
            part = slice(i * tokens, (i + 1) * tokens)
            s = lax.dot_general(keys[part], q, NT, preferred_element_type=F32)
            w = jnp.exp2(s + bias[i])
            total = total + jnp.sum(w, axis=0, keepdims=True)
            wt_ref[part, lanes] = w.astype(BF16)
        o = jnp.dot(values_t, wt_ref[:, lanes], preferred_element_type=F32)
        out = slice(h * HEAD_DIM, (h + 1) * HEAD_DIM)
        if first:
            acc_ref[out, :] = o
            den_ref[h : h + 1, :] = total
        else:
            acc_ref[out, :] = acc_in[out, :] + o
            den_ref[h : h + 1, :] = den_in[h : h + 1, :] + total


def mid_kernel(acc_ref, den_ref, dot_ref, stat_ref, own_ref, send_ref):
    rows = den_ref.shape[1] // 2
    for h in range(GROUP):
        out = slice(h * HEAD_DIM, (h + 1) * HEAD_DIM)
        den = den_ref[h : h + 1, :]
        part = acc_ref[out, :] / jnp.where(den > 0, den, 1.0)
        stat_ref[h : h + 1, :] = den
        stat_ref[GROUP + h : GROUP + h + 1, :] = jnp.sum(
            part * dot_ref[out, :].astype(F32), axis=0, keepdims=True
        )
        own_ref[out, :] = part[:, :rows]
        send_ref[out, :] = part[:, rows:].astype(BF16)


def join_stats(mine_ref, theirs_ref):
    rows = mine_ref.shape[1] // 2
    theirs = jnp.concatenate([theirs_ref[:, rows:], theirs_ref[:, :rows]], axis=1)
    den_a, den_b = mine_ref[:GROUP, :], theirs[:GROUP, :]
    den = den_a + den_b
    inv = 1.0 / jnp.where(den > 0, den, 1.0)
    share_a, share_b = den_a * inv, den_b * inv
    delta = share_a * mine_ref[GROUP:, :] + share_b * theirs[GROUP:, :]
    return inv, delta, share_a, share_b


def bwd_kernel(wt_ref, kv_ref, qh_ref, do_ref, mine_ref, theirs_ref, out_ref, ds_ref, dn_ref):
    rows = qh_ref.shape[0] // GROUP
    inv, delta, _, _ = join_stats(mine_ref, theirs_ref)
    delta = delta * inv
    columns = inv.T
    values = kv_ref[:, HEAD_DIM:]
    for h in range(GROUP):
        at = slice(h * rows, (h + 1) * rows)
        dn = (do_ref[at, :].astype(F32) * columns[:, h : h + 1]).astype(BF16)
        dn_ref[at, :] = dn
        dp = lax.dot_general(values, dn, NT, preferred_element_type=F32)
        ds = wt_ref[:, at].astype(F32) * (dp - delta[h : h + 1, :])
        ds_ref[:, at] = ds.astype(BF16)
    dv = jnp.dot(wt_ref[...], dn_ref[...], preferred_element_type=F32)
    dk = jnp.dot(ds_ref[...], qh_ref[...], preferred_element_type=F32)
    out_ref[:, :HEAD_DIM] = dk.astype(BF16)
    out_ref[:, HEAD_DIM:] = dv.astype(BF16)


def join_kernel(own_ref, got_ref, mine_ref, theirs_ref, out_ref):
    rows = own_ref.shape[1]
    _, _, share_a, share_b = join_stats(mine_ref, theirs_ref)
    for h in range(GROUP):
        lanes = slice(h * HEAD_DIM, (h + 1) * HEAD_DIM)
        joined = own_ref[lanes, :] * share_a[h : h + 1, :rows] + got_ref[lanes, :].astype(
            F32
        ) * share_b[h : h + 1, :rows]
        out_ref[:, lanes] = joined.T.astype(BF16)


def local(mesh, queries, grad_out, states, kv_weight, query_gain, key_gain, row_tiles):
    seq, grp, heads = mesh.shape["seq"], mesh.shape["grp"], mesh.shape["head"]
    outer = seq // (CORES * MID)
    rows = queries.shape[0]
    tokens = states.shape[0]
    both = 2 * rows
    gain = key_gain.reshape(1, HEAD_DIM)

    def device(a, m, c, g):
        return (((a % outer) * MID + m % MID) * CORES + c % CORES) * grp + g % grp

    def shift(x, da=0, dm=0, dc=0, dg=0):
        perm = [
            (device(a, m, c, g), device(a + da, m + dm, c + dc, g + dg))
            for a in range(outer)
            for m in range(MID)
            for c in range(CORES)
            for g in range(grp)
        ]
        return lax.ppermute(x, AXES, perm)

    sds = jax.ShapeDtypeStruct

    limit = jnp.repeat(row_tiles.T, TILES, axis=0)
    tile = jnp.tile(jnp.arange(TILES, dtype=row_tiles.dtype), IMAGES)[:, None]
    bias = jnp.where(tile < limit, 0.0, HIDDEN).astype(F32)
    q_par = shift(queries, dc=1)
    d_par = shift(grad_out, dc=1)
    b_par = shift(bias, dc=1)

    if heads == 1:
        kv, raw = project(states, kv_weight, gain)
    else:
        partial_value = jnp.dot(states, kv_weight, preferred_element_type=F32)
        raw = lax.psum_scatter(partial_value, "head", scatter_dimension=1, tiled=True)
        kv = norm_kv(raw, gain)

    qh, do, dot = call(
        prep_kernel,
        (
            sds((GROUP * both, HEAD_DIM), BF16),
            sds((GROUP * both, HEAD_DIM), BF16),
            sds((GROUP * HEAD_DIM, both), BF16),
        ),
        5,
        flops=both * GROUP * HEAD_DIM * 8,
        nbytes=both * GROUP * HEAD_DIM * 10,
    )(queries, q_par, grad_out, d_par, query_gain.reshape(1, HEAD_DIM))

    blocks = [kv] + [shift(kv, da=-d) for d in range(1, outer)]
    here = jnp.concatenate(blocks, axis=0)
    quads = [(m, g) for m in range(MID) for g in range(grp)]
    quads.sort(key=lambda q: (q[0] > 0) + (q[1] > 0))
    parts = [here if q == (0, 0) else shift(here, dm=-q[0], dg=-q[1]) for q in quads]

    seq_at, grp_at = lax.axis_index("seq"), lax.axis_index("grp")
    a_at, m_at, c_at = seq_at // (MID * CORES), (seq_at // CORES) % MID, seq_at % CORES
    span = outer * tokens
    group_rows = GROUP * both
    work = 2 * span * group_rows * HEAD_DIM

    acc = den = None
    weights = []
    for q, kv_part in zip(quads, parts):
        tiles = jnp.stack(
            [device(a_at + d, m_at + q[0], c_at, grp_at + q[1]) * tokens // TILE_TOK for d in range(outer)]
        ).astype(jnp.int32)
        first = acc is None
        carry = () if first else (acc, den)
        wt, acc, den = call(
            functools.partial(fwd_kernel, first, tokens),
            (
                sds((span, group_rows), BF16),
                sds((GROUP * HEAD_DIM, both), F32),
                sds((GROUP, both), F32),
            ),
            5 + len(carry),
            smem=1,
            flops=2 * work,
            nbytes=2 * span * group_rows,
            exps=span * group_rows,
        )(tiles, kv_part, qh, bias, b_par, *carry)
        weights.append(wt)

    stat, own, send = call(
        mid_kernel,
        (
            sds((2 * GROUP, both), F32),
            sds((GROUP * HEAD_DIM, rows), F32),
            sds((GROUP * HEAD_DIM, rows), BF16),
        ),
        3,
        flops=4 * GROUP * HEAD_DIM * both,
        nbytes=8 * GROUP * HEAD_DIM * both,
    )(acc, den, dot)
    stat_par = shift(stat, dc=1)
    got = shift(send, dc=1)

    grads = []
    for q, kv_part, wt in reversed(list(zip(quads, parts, weights))):
        part = call(
            bwd_kernel,
            sds((span, 2 * HEAD_DIM), BF16),
            6,
            flops=3 * work,
            nbytes=2 * span * group_rows,
            scratch=(pltpu.VMEM((span, group_rows), BF16), pltpu.VMEM((group_rows, HEAD_DIM), BF16)),
        )(wt, kv_part, qh, do, stat, stat_par)
        grads.append(part if q == (0, 0) else shift(part, dm=q[0], dg=q[1]))

    attended = call(
        join_kernel,
        sds((rows, GROUP * HEAD_DIM), BF16),
        4,
        flops=4 * GROUP * HEAD_DIM * rows,
        nbytes=8 * GROUP * HEAD_DIM * rows,
    )(own, got, stat, stat_par)

    total = sum(g.astype(F32) for g in grads).astype(BF16)
    pieces = [total[d * tokens : (d + 1) * tokens] for d in range(outer)]
    summed = pieces[0].astype(F32) + sum(
        shift(pieces[d], da=d).astype(F32) for d in range(1, outer)
    )

    keys_raw = raw[:, :HEAD_DIM]
    key_rms = root_mean(keys_raw)
    g = summed[:, :HEAD_DIM] * (gain / LOG2E)
    raw_grad = g / key_rms - keys_raw * jnp.mean(g * keys_raw, axis=-1, keepdims=True) / key_rms**3
    kv_grad = jnp.concatenate([raw_grad, summed[:, HEAD_DIM:]], axis=1)
    return attended, kv_grad


def solution(mesh):
    return jax.shard_map(
        functools.partial(local, mesh),
        mesh=mesh,
        in_specs=(
            P(AXES, "head"),
            P(AXES, "head"),
            P(AXES, "head"),
            P("head", None),
            P(),
            P(),
            P(AXES, None),
        ),
        out_specs=(P(AXES, "head"), P(AXES, "head")),
        check_vma=False,
    )
```

```python
import functools
import math

import jax
import jax.numpy as jnp
from jax import lax
from jax.experimental import pallas as pl
from jax.experimental.pallas import tpu as pltpu
from jax.sharding import PartitionSpec as P

HEAD_DIM = 128
GROUP = 8
IMAGES = 2
TILES = 4
TILE_TOK = 512
CORES = 2
MID = 2
EPS = 1e-05
LOG2E = 1.0 / math.log(2.0)
HIDDEN = -1e30
F32 = jnp.float32
BF16 = jnp.bfloat16
AXES = ("seq", "grp")

VMEM_BYTES = 16 << 20


NT = (((1,), (1,)), ((), ()))


def call(kernel, outs, n_in, flops=0, nbytes=0, exps=0, scratch=(), smem=0, **kw):
    vmem = pl.BlockSpec(memory_space=pltpu.VMEM)
    return pl.pallas_call(
        kernel,
        out_shape=outs,
        in_specs=[pl.BlockSpec(memory_space=pltpu.SMEM)] * smem + [vmem] * (n_in - smem),
        out_specs=jax.tree.map(lambda _: vmem, outs),
        scratch_shapes=scratch,
        cost_estimate=pl.CostEstimate(flops=flops, bytes_accessed=nbytes, transcendentals=exps),
        compiler_params=pltpu.CompilerParams(vmem_limit_bytes=VMEM_BYTES),
        **kw,
    )


def root_mean(values):
    return jnp.sqrt(jnp.mean(values * values, axis=-1, keepdims=True) + EPS)


def norm_kv(proj, gain):
    raw = proj[:, :HEAD_DIM]
    keys = raw / root_mean(raw) * gain
    return jnp.concatenate([keys.astype(BF16), proj[:, HEAD_DIM:].astype(BF16)], axis=1)


def project_kernel(states_ref, weight_ref, gain_ref, kv_ref, raw_ref):
    step = pl.program_id(0)

    @pl.when(step == 0)
    def _():
        raw_ref[...] = jnp.zeros_like(raw_ref)

    raw_ref[...] += jnp.dot(states_ref[...], weight_ref[...], preferred_element_type=F32)

    @pl.when(step == pl.num_programs(0) - 1)
    def _():
        kv_ref[...] = norm_kv(raw_ref[...], gain_ref[...])


def project(states, weight, gain):
    tokens, depth = states.shape
    width = weight.shape[1]
    block = min(depth, 1024)
    return pl.pallas_call(
        project_kernel,
        out_shape=(
            jax.ShapeDtypeStruct((tokens, width), BF16),
            jax.ShapeDtypeStruct((tokens, width), F32),
        ),
        grid=(depth // block,),
        in_specs=[
            pl.BlockSpec((tokens, block), lambda i: (0, i)),
            pl.BlockSpec((block, width), lambda i: (i, 0)),
            pl.BlockSpec((1, HEAD_DIM), lambda i: (0, 0)),
        ],
        out_specs=(
            pl.BlockSpec((tokens, width), lambda i: (0, 0)),
            pl.BlockSpec((tokens, width), lambda i: (0, 0)),
        ),
        cost_estimate=pl.CostEstimate(
            flops=2 * tokens * depth * width,
            bytes_accessed=2 * (tokens + width) * depth,
            transcendentals=0,
        ),
        compiler_params=pltpu.CompilerParams(vmem_limit_bytes=VMEM_BYTES),
    )(states, weight, gain)


def prep_kernel(q_own, q_par, d_own, d_par, gain_ref, qh_ref, do_ref, dot_ref):
    rows = q_own.shape[0]
    scale = LOG2E / math.sqrt(HEAD_DIM)
    gain = gain_ref[...] * scale
    for part, (q_ref, d_ref) in enumerate(((q_own, d_own), (q_par, d_par))):
        for h in range(GROUP):
            lanes = slice(h * HEAD_DIM, (h + 1) * HEAD_DIM)
            at = h * 2 * rows + part * rows
            q = q_ref[:, lanes].astype(F32)
            qh_ref[at : at + rows, :] = (q / root_mean(q) * gain).astype(BF16)
            d = d_ref[:, lanes]
            do_ref[at : at + rows, :] = d
            dot_ref[lanes, part * rows : (part + 1) * rows] = d.astype(F32).T.astype(BF16)


def fwd_kernel(first, tokens, tiles_ref, kv_ref, qh_ref, b_own, b_par, *refs):
    if first:
        wt_ref, acc_ref, den_ref = refs
    else:
        acc_in, den_in, wt_ref, acc_ref, den_ref = refs
    rows = qh_ref.shape[0] // GROUP
    keys = kv_ref[:, :HEAD_DIM]
    values_t = kv_ref[:, HEAD_DIM:].astype(F32).T.astype(BF16)
    blocks = kv_ref.shape[0] // tokens
    bias = []
    for i in range(blocks):
        row = pl.ds(tiles_ref[i], 1)
        bias.append(jnp.concatenate([b_own[row, :], b_par[row, :]], axis=1))
    for h in range(GROUP):
        q = qh_ref[h * rows : (h + 1) * rows, :]
        lanes = slice(h * rows, (h + 1) * rows)
        total = jnp.zeros((1, rows), F32)
        for i in range(blocks):
            part = slice(i * tokens, (i + 1) * tokens)
            s = lax.dot_general(keys[part], q, NT, preferred_element_type=F32)
            w = jnp.exp2(s + bias[i])
            total = total + jnp.sum(w, axis=0, keepdims=True)
            wt_ref[part, lanes] = w.astype(BF16)
        o = jnp.dot(values_t, wt_ref[:, lanes], preferred_element_type=F32)
        out = slice(h * HEAD_DIM, (h + 1) * HEAD_DIM)
        if first:
            acc_ref[out, :] = o
            den_ref[h : h + 1, :] = total
        else:
            acc_ref[out, :] = acc_in[out, :] + o
            den_ref[h : h + 1, :] = den_in[h : h + 1, :] + total


def mid_kernel(acc_ref, den_ref, dot_ref, stat_ref, own_ref, send_ref):
    rows = den_ref.shape[1] // 2
    for h in range(GROUP):
        out = slice(h * HEAD_DIM, (h + 1) * HEAD_DIM)
        den = den_ref[h : h + 1, :]
        part = acc_ref[out, :] / jnp.where(den > 0, den, 1.0)
        stat_ref[h : h + 1, :] = den
        stat_ref[GROUP + h : GROUP + h + 1, :] = jnp.sum(
            part * dot_ref[out, :].astype(F32), axis=0, keepdims=True
        )
        own_ref[out, :] = part[:, :rows]
        send_ref[out, :] = part[:, rows:].astype(BF16)


def join_stats(mine_ref, theirs_ref):
    rows = mine_ref.shape[1] // 2
    theirs = jnp.concatenate([theirs_ref[:, rows:], theirs_ref[:, :rows]], axis=1)
    den_a, den_b = mine_ref[:GROUP, :], theirs[:GROUP, :]
    den = den_a + den_b
    inv = 1.0 / jnp.where(den > 0, den, 1.0)
    share_a, share_b = den_a * inv, den_b * inv
    delta = share_a * mine_ref[GROUP:, :] + share_b * theirs[GROUP:, :]
    return inv, delta, share_a, share_b


def bwd_kernel(wt_ref, kv_ref, qh_ref, do_ref, mine_ref, theirs_ref, out_ref, ds_ref, dn_ref):
    rows = qh_ref.shape[0] // GROUP
    inv, delta, _, _ = join_stats(mine_ref, theirs_ref)
    delta = delta * inv
    columns = inv.T
    values = kv_ref[:, HEAD_DIM:]
    for h in range(GROUP):
        at = slice(h * rows, (h + 1) * rows)
        dn = (do_ref[at, :].astype(F32) * columns[:, h : h + 1]).astype(BF16)
        dn_ref[at, :] = dn
        dp = lax.dot_general(values, dn, NT, preferred_element_type=F32)
        ds = wt_ref[:, at].astype(F32) * (dp - delta[h : h + 1, :])
        ds_ref[:, at] = ds.astype(BF16)
    dv = jnp.dot(wt_ref[...], dn_ref[...], preferred_element_type=F32)
    dk = jnp.dot(ds_ref[...], qh_ref[...], preferred_element_type=F32)
    out_ref[:, :HEAD_DIM] = dk.astype(BF16)
    out_ref[:, HEAD_DIM:] = dv.astype(BF16)


def join_kernel(own_ref, got_ref, mine_ref, theirs_ref, out_ref):
    rows = own_ref.shape[1]
    _, _, share_a, share_b = join_stats(mine_ref, theirs_ref)
    for h in range(GROUP):
        lanes = slice(h * HEAD_DIM, (h + 1) * HEAD_DIM)
        joined = own_ref[lanes, :] * share_a[h : h + 1, :rows] + got_ref[lanes, :].astype(
            F32
        ) * share_b[h : h + 1, :rows]
        out_ref[:, lanes] = joined.T.astype(BF16)


def local(mesh, queries, grad_out, states, kv_weight, query_gain, key_gain, row_tiles):
    seq, grp, heads = mesh.shape["seq"], mesh.shape["grp"], mesh.shape["head"]
    outer = seq // (CORES * MID)
    rows = queries.shape[0]
    tokens = states.shape[0]
    both = 2 * rows
    gain = key_gain.reshape(1, HEAD_DIM)

    def device(a, m, c, g):
        return (((a % outer) * MID + m % MID) * CORES + c % CORES) * grp + g % grp

    def shift(x, da=0, dm=0, dc=0, dg=0):
        perm = [
            (device(a, m, c, g), device(a + da, m + dm, c + dc, g + dg))
            for a in range(outer)
            for m in range(MID)
            for c in range(CORES)
            for g in range(grp)
        ]
        return lax.ppermute(x, AXES, perm)

    sds = jax.ShapeDtypeStruct

    limit = jnp.repeat(row_tiles.T, TILES, axis=0)
    tile = jnp.tile(jnp.arange(TILES, dtype=row_tiles.dtype), IMAGES)[:, None]
    bias = jnp.where(tile < limit, 0.0, HIDDEN).astype(F32)
    q_par = shift(queries, dc=1)
    d_par = shift(grad_out, dc=1)
    b_par = shift(bias, dc=1)

    if heads == 1:
        kv, raw = project(states, kv_weight, gain)
    else:
        partial_value = jnp.dot(states, kv_weight, preferred_element_type=F32)
        raw = lax.psum_scatter(partial_value, "head", scatter_dimension=1, tiled=True)
        kv = norm_kv(raw, gain)

    qh, do, dot = call(
        prep_kernel,
        (
            sds((GROUP * both, HEAD_DIM), BF16),
            sds((GROUP * both, HEAD_DIM), BF16),
            sds((GROUP * HEAD_DIM, both), BF16),
        ),
        5,
        flops=both * GROUP * HEAD_DIM * 8,
        nbytes=both * GROUP * HEAD_DIM * 10,
    )(queries, q_par, grad_out, d_par, query_gain.reshape(1, HEAD_DIM))

    blocks = [kv] + [shift(kv, da=-d) for d in range(1, outer)]
    here = jnp.concatenate(blocks, axis=0)
    quads = [(m, g) for m in range(MID) for g in range(grp)]
    quads.sort(key=lambda q: (q[0] > 0) + (q[1] > 0))
    parts = [here if q == (0, 0) else shift(here, dm=-q[0], dg=-q[1]) for q in quads]

    seq_at, grp_at = lax.axis_index("seq"), lax.axis_index("grp")
    a_at, m_at, c_at = seq_at // (MID * CORES), (seq_at // CORES) % MID, seq_at % CORES
    span = outer * tokens
    group_rows = GROUP * both
    work = 2 * span * group_rows * HEAD_DIM

    acc = den = None
    weights = []
    for q, kv_part in zip(quads, parts):
        tiles = jnp.stack(
            [device(a_at + d, m_at + q[0], c_at, grp_at + q[1]) * tokens // TILE_TOK for d in range(outer)]
        ).astype(jnp.int32)
        first = acc is None
        carry = () if first else (acc, den)
        wt, acc, den = call(
            functools.partial(fwd_kernel, first, tokens),
            (
                sds((span, group_rows), BF16),
                sds((GROUP * HEAD_DIM, both), F32),
                sds((GROUP, both), F32),
            ),
            5 + len(carry),
            smem=1,
            flops=2 * work,
            nbytes=2 * span * group_rows,
            exps=span * group_rows,
        )(tiles, kv_part, qh, bias, b_par, *carry)
        weights.append(wt)

    stat, own, send = call(
        mid_kernel,
        (
            sds((2 * GROUP, both), F32),
            sds((GROUP * HEAD_DIM, rows), F32),
            sds((GROUP * HEAD_DIM, rows), BF16),
        ),
        3,
        flops=4 * GROUP * HEAD_DIM * both,
        nbytes=8 * GROUP * HEAD_DIM * both,
    )(acc, den, dot)
    stat_par = shift(stat, dc=1)
    got = shift(send, dc=1)

    grads = []
    for q, kv_part, wt in reversed(list(zip(quads, parts, weights))):
        part = call(
            bwd_kernel,
            sds((span, 2 * HEAD_DIM), BF16),
            6,
            flops=3 * work,
            nbytes=2 * span * group_rows,
            scratch=(pltpu.VMEM((span, group_rows), BF16), pltpu.VMEM((group_rows, HEAD_DIM), BF16)),
        )(wt, kv_part, qh, do, stat, stat_par)
        grads.append(part if q == (0, 0) else shift(part, dm=q[0], dg=q[1]))

    attended = call(
        join_kernel,
        sds((rows, GROUP * HEAD_DIM), BF16),
        4,
        flops=4 * GROUP * HEAD_DIM * rows,
        nbytes=8 * GROUP * HEAD_DIM * rows,
    )(own, got, stat, stat_par)

    total = sum(g.astype(F32) for g in grads).astype(BF16)
    pieces = [total[d * tokens : (d + 1) * tokens] for d in range(outer)]
    summed = pieces[0].astype(F32) + sum(
        shift(pieces[d], da=d).astype(F32) for d in range(1, outer)
    )

    keys_raw = raw[:, :HEAD_DIM]
    key_rms = root_mean(keys_raw)
    g = summed[:, :HEAD_DIM] * (gain / LOG2E)
    raw_grad = g / key_rms - keys_raw * jnp.mean(g * keys_raw, axis=-1, keepdims=True) / key_rms**3
    kv_grad = jnp.concatenate([raw_grad, summed[:, HEAD_DIM:]], axis=1)
    return attended, kv_grad


def solution(mesh):
    return jax.shard_map(
        functools.partial(local, mesh),
        mesh=mesh,
        in_specs=(
            P(AXES, "head"),
            P(AXES, "head"),
            P(AXES, "head"),
            P("head", None),
            P(),
            P(),
            P(AXES, None),
        ),
        out_specs=(P(AXES, "head"), P(AXES, "head")),
        check_vma=False,
    )
```
